32 devices in a mesh: dp: 2 (over y), space: 16 (over z, x, core).
Axes of the slice: x: 2, y: 2, z: 4, core: 2. Of those that a mesh axis runs over, the one named last changes fastest.
Arguments:
- volumes: bfloat16 [2, 64, 32, 4096], P('dp', 'space'), may hold values from -6 to 6
- first_filter: bfloat16 [3, 3, 3, 64, 128], replicated, may hold values from -0.15625 to 0.15625
- second_filter: bfloat16 [3, 3, 3, 128, 128], replicated, may hold values from -0.109375 to 0.109375
- upstream_grad: bfloat16 [2, 16, 8, 16, 128], P('dp', 'space'), may hold values from -0.029907227 to 0.029907227
Outputs:
- second_out: bfloat16 [2, 16, 8, 16, 128], P('dp', 'space')
- first_grad: float32 [3, 3, 3, 64, 128], P(None, None, None, None, 'space')
- second_grad: float32 [3, 3, 3, 128, 128], P(None, None, None, 'space')
The draws below stay inside these ranges and needn't reach their ends.
All inputs are finite; a program needn't handle non-finite values.
Results may differ from the reference program's by a relative error of at most 0.01.
The reference program's roundings to bfloat16 on the way (of `hidden`, `grad_pre_two`, `grad_hidden` and `grad_pre_one`) count: a program that leaves them out, or rounds other values in their place, can miss the bound.
Values may be sent and summed in bfloat16 or wider, within the bound.
A program may use at most 64 MiB of HBM per device.

```python
import jax
import jax.numpy as jnp
from jax import lax

C0 = 64
C1 = 128
HEIGHT = 32
WIDTH = 64
B = 2
DEPTH = 64


def block_scale(own_key, dims, split, low, high):
    factor_of = 1.0
    for axis_at, blocks in split:
        heights = jax.random.uniform(jax.random.fold_in(jax.random.fold_in(own_key, 6), axis_at), (blocks,), jnp.float32, low / len(split), high / len(split))
        factor_of = factor_of * jnp.repeat(jnp.exp(heights), dims[axis_at] // blocks).reshape((-1,) + (1,) * (len(dims) - 1 - axis_at))
    return factor_of


def centred(rng, shape, scale, bound, shards=(), dtype=jnp.bfloat16):
    entries = scale * jax.random.normal(rng, shape, jnp.float32)
    if shards:
        entries = entries * block_scale(rng, shape, shards, -0.22, 0.18)
    return jnp.clip(entries, -bound, bound).astype(dtype)


def setup_inputs(seed: int = 0) -> dict:
    streams_of = jax.random.split(jax.random.key(seed), 5)
    return {
        "volumes": centred(streams_of[0], (B, DEPTH, HEIGHT, WIDTH * C0), 1.0, 6.0, ((0, 2), (1, 16))),
        "first_filter": centred(streams_of[1], (3, 3, 3, C0, C1), (27 * C0) ** -0.5, 0.15625),
        "second_filter": centred(streams_of[2], (3, 3, 3, C1, C1), (27 * C1) ** -0.5, 0.109375),
        "upstream_grad": centred(streams_of[3], (B, DEPTH // 4, HEIGHT // 4, WIDTH // 4, C1), 0.005, 0.029907227, ((0, 2), (1, 16))),
    }


SLOPE = 0.3

def leaky_relu(values):
    return jnp.where(values > 0, values, SLOPE * values)

def extract(volume, depth_pad):
    padded = jnp.pad(volume, ((0, 0), depth_pad, (1, 1), (1, 1), (0, 0)))
    depth_out = (padded.shape[1] - 3) // 2 + 1
    height_out = (padded.shape[2] - 3) // 2 + 1
    width_out = (padded.shape[3] - 3) // 2 + 1
    pieces = []
    for i in range(3):
        for j in range(3):
            for k in range(3):
                pieces.append(padded[:, i:i + 2 * depth_out - 1:2, j:j + 2 * height_out - 1:2, k:k + 2 * width_out - 1:2, :])
    return jnp.concatenate(pieces, axis=-1)

def spread(grads, shape, depth_pad):
    base = jnp.zeros(shape, jnp.float32)
    unused, pullback = jax.vjp(lambda volume: extract(volume, depth_pad), base)
    return pullback(grads)[0]

def flatten(values):
    return values.reshape(-1, values.shape[-1])

def contract_rows(left, right):
    return lax.dot_general(left, right, (((0,), (0,)), ((), ())), preferred_element_type=jnp.float32)

def reference(volumes, first_filter, second_filter, upstream_grad):
    first_flat = first_filter.reshape(27 * C0, C1)
    second_flat = second_filter.reshape(27 * C1, C1)

    def per_sample(carry, inputs):
        grad_one, grad_two = carry
        sample_volume, sample_grad = inputs
        volume_view = sample_volume.reshape(1, DEPTH, HEIGHT, WIDTH, C0)
        columns_one = extract(volume_view, (1, 1))
        shape_one = columns_one.shape[:-1]
        pre_one = jnp.dot(flatten(columns_one), first_flat, preferred_element_type=jnp.float32)
        hidden = leaky_relu(pre_one).astype(jnp.bfloat16).reshape(shape_one + (C1,))
        columns_two = extract(hidden, (1, 1))
        shape_two = columns_two.shape[:-1]
        pre_two = jnp.dot(flatten(columns_two), second_flat, preferred_element_type=jnp.float32).reshape(shape_two + (C1,))
        second_out = leaky_relu(pre_two).astype(jnp.bfloat16)
        grad_pre_two = (sample_grad[None].astype(jnp.float32) * jnp.where(pre_two > 0, 1.0, SLOPE)).astype(jnp.bfloat16)
        grad_two = grad_two + contract_rows(flatten(columns_two), flatten(grad_pre_two))
        grad_columns = lax.dot_general(flatten(grad_pre_two), second_flat, (((1,), (1,)), ((), ())), preferred_element_type=jnp.float32)
        grad_hidden = spread(grad_columns.reshape(shape_two + (27 * C1,)), hidden.shape, (1, 1)).astype(jnp.bfloat16)
        grad_pre_one = (grad_hidden.astype(jnp.float32) * jnp.where(hidden > 0, 1.0, SLOPE)).astype(jnp.bfloat16)
        grad_one = grad_one + contract_rows(flatten(columns_one), flatten(grad_pre_one))
        return ((grad_one, grad_two), second_out[0])
    start = (jnp.zeros((27 * C0, C1), jnp.float32), jnp.zeros((27 * C1, C1), jnp.float32))
    (grad_one, grad_two), second_out = lax.scan(per_sample, start, (volumes, upstream_grad))
    return (second_out, grad_one.reshape(3, 3, 3, C0, C1), grad_two.reshape(3, 3, 3, C1, C1))
```

```python
import functools

import jax
import jax.numpy as jnp
from jax import lax
from jax.experimental import pallas as pl
from jax.experimental.pallas import tpu as pltpu
from jax.sharding import PartitionSpec as P

SLOPE = 0.3
F32, BF16 = jnp.float32, jnp.bfloat16
MESH = pl.DeviceIdType.MESH
GROUP = 8


def dot(lhs, rhs, contract=((1,), (0,))):
    return lax.dot_general(lhs, rhs, (contract, ((), ())), preferred_element_type=F32)


def log2(n):
    return n.bit_length() - 1


def reversed_bits(value, bits):
    return sum(((value >> k) & 1) << (bits - 1 - k) for k in range(bits))


def stages_of(spaces, samples, groups):
    group_bits, space_bits = log2(groups), log2(spaces)
    extra = space_bits - group_bits
    stages = [("space", extra + k, True) for k in range(group_bits)]
    stages += [("space", k, False) for k in range(extra)]
    stages += [("dp", k, False) for k in range(log2(samples))]
    return stages


def shift_down(values, axis=1):
    at = lax.broadcasted_iota(jnp.int32, values.shape, axis)
    return jnp.where(at == 0, 0.0, pltpu.roll(values, 1, axis))


def shift_up(values, axis=1):
    size = values.shape[axis]
    at = lax.broadcasted_iota(jnp.int32, values.shape, axis)
    return jnp.where(at == size - 1, 0.0, pltpu.roll(values, size - 1, axis))


def rows_back(values):
    return jnp.concatenate([jnp.zeros_like(values[:1]), values[:-1]], axis=0)


def rows_ahead(values):
    return jnp.concatenate([values[1:], jnp.zeros_like(values[:1])], axis=0)


def flat(values):
    return values.reshape(-1, values.shape[-1])


def slope_of(values):
    return jnp.where(values > 0, 1.0, SLOPE)


class Reduction:
    def __init__(self, stages, sums, received, sends, receives, out):
        self.stages, self.sums, self.received = stages, sums, received
        self.sends, self.receives, self.out = sends, receives, out
        self.copy = None

    def start(self, t):
        axis, bit, halves = self.stages[t]
        me = lax.axis_index(axis)
        own = (me // (1 << bit)) % 2
        partner = me + (1 - 2 * own) * (1 << bit)
        held = self.sums[t]
        count = held.shape[0]
        if halves:
            source = held.at[pl.ds((1 - own) * (count // 2), count // 2)]
        else:
            source = held
        self.copy = pltpu.make_async_remote_copy(
            src_ref=source,
            dst_ref=self.received[t],
            send_sem=self.sends.at[t],
            recv_sem=self.receives.at[t],
            device_id={axis: partner},
            device_id_type=MESH,
        )
        self.copy.start()
        self.own, self.halves = own, halves

    def finish(self, t):
        self.copy.wait()
        held = self.sums[t]
        count = held.shape[0]
        if self.halves:
            mine = held[pl.ds(self.own * (count // 2), count // 2)]
        else:
            mine = held[...]
        total = mine.astype(F32) + self.received[t][...].astype(F32)
        if t + 1 < len(self.stages):
            self.sums[t + 1][...] = total.astype(BF16)
            self.start(t + 1)
        else:
            self.out[...] = total[0]


def kernel(stages, spaces, groups, vol, w1, w2, up, second_out, out1, out2, *scratch):
    count = len(stages)
    (vol_rim, hidden_send, hidden_rim, hf, g2_send, g2_next, gf, halo_send, halo_recv) = scratch[:9]
    sums2, recv2 = scratch[9 : 9 + count], scratch[9 + count : 9 + 2 * count]
    sums1, recv1 = scratch[9 + 2 * count : 9 + 3 * count], scratch[9 + 3 * count : 9 + 4 * count]
    send2, got2, send1, got1 = scratch[9 + 4 * count :]
    red2 = Reduction(stages, sums2, recv2, send2, got2, out2)
    red1 = Reduction(stages, sums1, recv1, send1, got1, out1)
    me = lax.axis_index("space")
    first, last = me == 0, me == spaces - 1
    bits = log2(groups)

    barrier = pltpu.get_barrier_semaphore()
    for axis, bit, _ in stages:
        at = lax.axis_index(axis)
        partner = at + (1 - 2 * ((at // (1 << bit)) % 2)) * (1 << bit)
        pl.semaphore_signal(barrier, inc=1, device_id={axis: partner}, device_id_type=MESH)

    @pl.when(me > 0)
    def _():
        pl.semaphore_signal(barrier, inc=1, device_id={"space": me - 1}, device_id_type=MESH)

    @pl.when(me < spaces - 1)
    def _():
        pl.semaphore_signal(barrier, inc=1, device_id={"space": me + 1}, device_id_type=MESH)

    ends = jnp.where(first, 1, 0) + jnp.where(last, 1, 0)
    pl.semaphore_wait(barrier, len(stages) + 2 - ends)

    def halo(index, source, target, by):
        return pltpu.make_async_remote_copy(
            src_ref=source,
            dst_ref=target,
            send_sem=halo_send.at[index],
            recv_sem=halo_recv.at[index],
            device_id={"space": me + by},
            device_id_type=MESH,
        )

    vol_copy = halo(0, vol.at[vol.shape[0] - 1], vol_rim, 1)
    hidden_copy = halo(1, hidden_send, hidden_rim, 1)
    g2_copy = halo(2, g2_send, g2_next, -1)

    @pl.when(me < spaces - 1)
    def _():
        vol_copy.start()

    taps1 = []
    for ab in range(9):
        zero = jnp.zeros_like(w1[0])
        right = jnp.concatenate([w1[3 * ab + 1], w1[3 * ab + 2]], axis=0)
        left = jnp.concatenate([zero, w1[3 * ab]], axis=0)
        taps1.append(jnp.concatenate([right, left], axis=1))
    w1_all = jnp.concatenate(taps1, axis=0)

    def vol_rows(plane, b):
        at = 1 if b == 0 else b - 1
        rows = vol_rim[:, at] if plane < 0 else vol[plane, :, at]
        return flat(rows_back(rows) if b == 0 else rows)

    def first_layer(p):
        columns = jnp.concatenate(
            [vol_rows(2 * p + a - 1, b) for a in range(3) for b in range(3)], axis=1
        )
        both = dot(columns, w1_all)
        cells = w1.shape[-1]
        height, width = vol.shape[1], vol.shape[3]
        here = both[:, :cells].reshape(height, width, cells)
        left = both[:, cells:].reshape(height, width, cells)
        pre = here + shift_down(left)
        return jnp.where(pre > 0, pre, SLOPE * pre).astype(BF16)

    def keep_hidden(plane, values):
        wide = values.astype(F32)
        hf[plane] = wide.reshape(hf.shape[1:])

    hidden = first_layer(1)
    hidden_send[...] = hidden

    @pl.when(me < spaces - 1)
    def _():
        hidden_copy.start()

    keep_hidden(2, hidden)

    @pl.when(me > 0)
    def _():
        vol_copy.wait_recv()

    @pl.when(first)
    def _():
        vol_rim[...] = jnp.zeros_like(vol_rim)

    keep_hidden(1, first_layer(0))

    @pl.when(me > 0)
    def _():
        hidden_copy.wait_recv()

    @pl.when(first)
    def _():
        hidden_rim[...] = jnp.zeros_like(hidden_rim)

    keep_hidden(0, hidden_rim[...])

    half_h, half_w = hf.shape[1], hf.shape[3] // 2

    def hidden_rows(plane, b, parity):
        at = 1 if b == 0 else b - 1
        rows = hf[plane, :, at, pl.ds(parity, half_w, stride=2), :]
        return flat(rows_back(rows) if b == 0 else rows)

    even = [hidden_rows(a, b, 0) for a in range(3) for b in range(3)]
    odd = [hidden_rows(a, b, 1) for a in range(3) for b in range(3)]
    pre = dot(
        jnp.concatenate([x.astype(BF16) for ab in range(9) for x in (even[ab], odd[ab])], axis=1),
        jnp.concatenate([w2[3 * ab + c] for ab in range(9) for c in (1, 2)], axis=0),
    )
    left = dot(
        jnp.concatenate([odd[ab].astype(BF16) for ab in range(9)], axis=1),
        jnp.concatenate([w2[3 * ab] for ab in range(9)], axis=0),
    )
    cells = w2.shape[-1]
    pre = pre + flat(shift_down(left.reshape(half_h, half_w, cells)))
    second_out[...] = jnp.where(pre > 0, pre, SLOPE * pre).astype(BF16)
    g2 = (up[...].astype(F32) * slope_of(pre)).astype(BF16)
    g2_send[...] = g2.reshape(half_h, half_w, cells)

    @pl.when(me > 0)
    def _():
        g2_copy.start()

    g2_wide = g2.astype(F32).reshape(half_h, half_w, cells)
    g2_ahead = shift_up(g2_wide).astype(BF16)
    g2_both = jnp.concatenate([g2, flat(g2_ahead)], axis=1)
    terms2 = []
    for ab in range(9):
        even_t = jnp.transpose(even[ab]).astype(BF16)
        odd_t = jnp.transpose(odd[ab]).astype(BF16)
        from_odd = dot(odd_t, g2_both)
        terms2 += [from_odd[:, cells:], dot(even_t, g2), from_odd[:, :cells]]

    def store_terms(target, terms):
        for k in range(0, len(terms), 2):
            one = terms[k].reshape(groups, GROUP, -1)
            two = terms[k + 1].reshape(groups, GROUP, -1) if k + 1 < len(terms) else jnp.zeros_like(one)
            pair = jnp.concatenate([one, two], axis=1).astype(BF16)
            for g in range(groups):
                target[reversed_bits(g, bits), pl.ds(k * GROUP, 2 * GROUP), :] = pair[g]

    store_terms(sums2[0], terms2)
    red2.start(0)

    @pl.when(me < spaces - 1)
    def _():
        g2_copy.wait_recv()

    @pl.when(last)
    def _():
        g2_next[...] = jnp.zeros_like(g2_next)

    planes = [(g2.reshape(half_h, half_w, cells), g2_ahead)]
    following = g2_next[...]
    planes.append((following, shift_up(following.astype(F32)).astype(BF16)))
    choices = {}
    for plane in range(2):
        for dr in range(2):
            values = planes[plane][dr]
            choices[plane, 0, dr] = flat(values)
            choices[plane, 1, dr] = flat(rows_ahead(values))
    reach = {0: [(1, 0)], 1: [(2, 0), (0, 1)]}
    for u in range(2):
        for v in range(2):
            for w in range(2):
                members = [
                    ((a * 3 + b) * 3 + c, (plane, dq, dr))
                    for a, plane in reach[u]
                    for b, dq in reach[v]
                    for c, dr in reach[w]
                ]
                grad = dot(
                    jnp.concatenate([choices[key] for _, key in members], axis=1),
                    jnp.concatenate([w2[tap] for tap, _ in members], axis=1),
                    ((1,), (1,)),
                )
                grad = grad.astype(BF16).astype(F32).reshape(half_h, half_w, cells)
                at = hf[1 + u, :, v, pl.ds(w, half_w, stride=2), :]
                grad = (grad * slope_of(at)).astype(BF16).astype(F32)
                gf[u, :, v, pl.ds(w, half_w, stride=2), :] = grad

    red2.finish(0)

    grad = gf[...].reshape(-1, gf.shape[3], cells)
    grad_t = jnp.concatenate(
        [jnp.transpose(flat(grad)).astype(BF16), jnp.transpose(flat(shift_up(grad))).astype(BF16)],
        axis=0,
    )
    pairs1, lefts1 = [], []
    for a in range(3):
        columns = jnp.concatenate(
            [
                jnp.concatenate([vol_rows(a - 1, b), vol_rows(a + 1, b)], axis=0)
                for b in range(3)
            ],
            axis=1,
        )
        both = dot(grad_t, columns)
        lanes = vol.shape[-1]
        for b in range(3):
            part = both[:, b * lanes : (b + 1) * lanes]
            pairs1.append(part[:cells])
            lefts1.append(part[cells:])
    lane = lax.broadcasted_iota(jnp.int32, lefts1[0].shape, 1)
    half = lanes // 2
    for k in range(0, 9, 2):
        upper = lefts1[k + 1] if k + 1 < 9 else jnp.zeros_like(lefts1[k])
        pairs1.append(jnp.where(lane < half, pltpu.roll(lefts1[k], half, 1), upper))
    store_terms(sums1[0], pairs1)
    red1.start(0)
    for t in range(count):
        if t + 1 < count:
            red2.finish(t + 1)
        red1.finish(t)

    @pl.when(me < spaces - 1)
    def _():
        vol_copy.wait_send()
        hidden_copy.wait_send()

    @pl.when(me > 0)
    def _():
        g2_copy.wait_send()


def local(volumes, first_filter, second_filter, upstream_grad, spaces, samples):
    _, depth, height, merged = volumes.shape
    c0, c1 = first_filter.shape[3:]
    width = merged // c0
    vol = volumes.reshape(depth, height // 2, 2, width // 2, 2 * c0)
    w1 = first_filter.reshape(27, c0, c1)
    w2 = second_filter.reshape(27, c1, c1)
    _, _, q, r, _ = upstream_grad.shape
    up = upstream_grad.reshape(q * r, c1)
    groups = min(c1 // GROUP, spaces)
    stages = stages_of(spaces, samples, groups)
    rows2, rows1 = 28 * GROUP, 14 * GROUP

    def buffers(rows):
        sums, received, size = [], [], groups
        for _, _, halves in stages:
            sums.append(pltpu.VMEM((size, rows, c1), BF16))
            size = size // 2 if halves else size
            received.append(pltpu.VMEM((size, rows, c1), BF16))
        return sums + received

    vmem = pl.BlockSpec(memory_space=pltpu.VMEM)
    dmas = pltpu.SemaphoreType.DMA((len(stages),))
    second_out, out1, out2 = pl.pallas_call(
        functools.partial(kernel, stages, spaces, groups),
        out_shape=(
            jax.ShapeDtypeStruct((q * r, c1), BF16),
            jax.ShapeDtypeStruct((rows1, c1), F32),
            jax.ShapeDtypeStruct((rows2, c1), F32),
        ),
        in_specs=[vmem] * 4,
        out_specs=(vmem,) * 3,
        scratch_shapes=[
            pltpu.VMEM((height // 2, 2, width // 2, 2 * c0), BF16),
            pltpu.VMEM((height // 2, width // 2, c1), BF16),
            pltpu.VMEM((height // 2, width // 2, c1), BF16),
            pltpu.VMEM((3, height // 4, 2, width // 2, c1), F32),
            pltpu.VMEM((q, r, c1), BF16),
            pltpu.VMEM((q, r, c1), BF16),
            pltpu.VMEM((2, height // 4, 2, width // 2, c1), F32),
            pltpu.SemaphoreType.DMA((3,)),
            pltpu.SemaphoreType.DMA((3,)),
            *buffers(rows2),
            *buffers(rows1),
            dmas,
            dmas,
            dmas,
            dmas,
        ],
        compiler_params=pltpu.CompilerParams(
            collective_id=0, has_side_effects=True, vmem_limit_bytes=50 * 1024 * 1024
        ),
    )(vol, w1, w2, up)

    own = c1 // spaces
    start = (lax.axis_index("space") % (GROUP // own)) * own if own < GROUP else 0
    units2 = out2.reshape(28, GROUP, c1)[:27]
    units1 = out1.reshape(14, GROUP, 2, c0)
    if own < GROUP:
        units2 = lax.dynamic_slice_in_dim(units2, start, own, 1)
        units1 = lax.dynamic_slice_in_dim(units1, start, own, 1)
    second_grad = units2.reshape(3, 3, 3, own, c1)
    centre = jnp.transpose(units1[:9], (0, 2, 3, 1))
    left = jnp.transpose(units1[9:], (0, 2, 3, 1)).reshape(10, c0, own)
    left = left[:9]
    first_grad = jnp.concatenate([left[:, None], centre], axis=1).reshape(3, 3, 3, c0, own)
    return second_out.reshape(1, 1, q, r, c1), first_grad, second_grad


def solution(mesh):
    placed = (P("dp", "space", None, None), P(), P(), P("dp", "space", None, None, None))
    body = functools.partial(local, spaces=mesh.shape["space"], samples=mesh.shape["dp"])
    return jax.shard_map(
        body,
        mesh=mesh,
        in_specs=placed,
        out_specs=(
            P("dp", "space", None, None, None),
            P(None, None, None, None, "space"),
            P(None, None, None, "space", None),
        ),
        check_vma=False,
    )
```

```python
import functools

import jax
import jax.numpy as jnp
from jax import lax
from jax.experimental import pallas as pl
from jax.experimental.pallas import tpu as pltpu
from jax.sharding import PartitionSpec as P

SLOPE = 0.3
F32, BF16 = jnp.float32, jnp.bfloat16
MESH = pl.DeviceIdType.MESH
GROUP = 8


def dot(lhs, rhs, contract=((1,), (0,))):
    return lax.dot_general(lhs, rhs, (contract, ((), ())), preferred_element_type=F32)


def log2(n):
    return n.bit_length() - 1


def bits_of(spaces, groups):
    extra = log2(spaces) - log2(groups)
    return list(range(extra, log2(spaces))), list(range(extra))


def straight(spaces, samples, groups):
    halving, shared = bits_of(spaces, groups)
    stages = [("space", k, "halve") for k in halving]
    stages += [("space", k, "full") for k in shared]
    return stages + [("dp", k, "full") for k in range(log2(samples))]


def samples_early(spaces, samples, groups):
    halving, shared = bits_of(spaces, groups)
    stages = [("space", k, "halve") for k in halving]
    stages.insert(1, ("dp", 0, "halve"))
    stages += [("space", k, "full") for k in shared]
    stages += [("dp", k, "full") for k in range(1, log2(samples))]
    return stages + [("dp", 0, "gather")]


def block_index(stages, group, low, sample_half):
    index = 0
    for axis, bit, kind in stages:
        if kind == "halve":
            value = (group >> (bit - low)) & 1 if axis == "space" else sample_half
            index = 2 * index + value
    return index


def split_of(stages):
    return 2 if stages[-1][2] == "gather" else 1


def shift_down(values, axis=1):
    at = lax.broadcasted_iota(jnp.int32, values.shape, axis)
    return jnp.where(at == 0, 0.0, pltpu.roll(values, 1, axis))


def shift_up(values, axis=1):
    size = values.shape[axis]
    at = lax.broadcasted_iota(jnp.int32, values.shape, axis)
    return jnp.where(at == size - 1, 0.0, pltpu.roll(values, size - 1, axis))


def rows_back(values):
    return jnp.concatenate([jnp.zeros_like(values[:1]), values[:-1]], axis=0)


def rows_ahead(values):
    return jnp.concatenate([values[1:], jnp.zeros_like(values[:1])], axis=0)


def flat(values):
    return values.reshape(-1, values.shape[-1])


def slope_of(values):
    return jnp.where(values > 0, 1.0, SLOPE)


class Reduction:
    def __init__(self, stages, scratch, out, out_row):
        count = len(stages)
        self.stages, self.out, self.out_row = stages, out, out_row
        self.sums, self.received = scratch[:count], scratch[count : 2 * count]
        self.sends, self.receives = scratch[2 * count :]
        self.copy = None

    def start(self, t):
        axis, bit, kind = self.stages[t]
        me = lax.axis_index(axis)
        own = (me // (1 << bit)) % 2
        partner = me + (1 - 2 * own) * (1 << bit)
        held = self.sums[t]
        source = held
        if kind == "halve":
            half = held.shape[0] // 2
            source = held.at[pl.ds((1 - own) * half, half)]
        self.copy = pltpu.make_async_remote_copy(
            src_ref=source,
            dst_ref=self.received[t],
            send_sem=self.sends.at[t],
            recv_sem=self.receives.at[t],
            device_id={axis: partner},
            device_id_type=MESH,
        )
        self.copy.start()
        self.own = own

    def finish(self, t):
        self.copy.wait()
        kind = self.stages[t][2]
        held = self.sums[t]
        rows = held.shape[1]
        if kind == "gather":
            for half, values in ((self.own, held), (1 - self.own, self.received[t])):
                at = pl.multiple_of(self.out_row + half * rows, GROUP)
                self.out[pl.ds(at, rows), :] = values[0].astype(F32)
            return
        if kind == "halve":
            half = held.shape[0] // 2
            mine = held[pl.ds(self.own * half, half)]
        else:
            mine = held[...]
        total = mine.astype(F32) + self.received[t][...].astype(F32)
        if t + 1 < len(self.stages):
            self.sums[t + 1][...] = total.astype(BF16)
            self.start(t + 1)
        else:
            self.out[pl.ds(self.out_row, rows), :] = total[0]


def kernel(plans, spaces, groups, vol, w1, w2, up, second_out, out1, out2, *scratch):
    (vol_rim, hidden_send, hidden_rim, hf, g2_send, g2_next, gf, sum1, halo_send, halo_recv) = scratch[:10]
    at, streams = 10, []
    for stages, tiles, first_tile, layer in plans:
        used = 2 * len(stages) + 2
        target = out2 if layer == 2 else sum1
        streams.append(Reduction(stages, scratch[at : at + used], target, first_tile * 2 * GROUP))
        at += used
    low = log2(spaces) - log2(groups)
    me = lax.axis_index("space")
    first, last = me == 0, me == spaces - 1

    barrier = pltpu.get_barrier_semaphore()
    partners = sorted({stage[:2] for plan in plans for stage in plan[0]})
    for axis, bit in partners:
        at = lax.axis_index(axis)
        partner = at + (1 - 2 * ((at // (1 << bit)) % 2)) * (1 << bit)
        pl.semaphore_signal(barrier, inc=1, device_id={axis: partner}, device_id_type=MESH)

    @pl.when(me > 0)
    def _():
        pl.semaphore_signal(barrier, inc=1, device_id={"space": me - 1}, device_id_type=MESH)

    @pl.when(me < spaces - 1)
    def _():
        pl.semaphore_signal(barrier, inc=1, device_id={"space": me + 1}, device_id_type=MESH)

    ends = jnp.where(first, 1, 0) + jnp.where(last, 1, 0)
    pl.semaphore_wait(barrier, len(partners) + 2 - ends)

    def halo(index, source, target, by):
        return pltpu.make_async_remote_copy(
            src_ref=source,
            dst_ref=target,
            send_sem=halo_send.at[index],
            recv_sem=halo_recv.at[index],
            device_id={"space": me + by},
            device_id_type=MESH,
        )

    vol_copy = halo(0, vol.at[vol.shape[0] - 1], vol_rim, 1)
    hidden_copy = halo(1, hidden_send, hidden_rim, 1)
    g2_copy = halo(2, g2_send, g2_next, -1)

    @pl.when(me < spaces - 1)
    def _():
        vol_copy.start()

    taps1 = []
    for ab in range(9):
        zero = jnp.zeros_like(w1[0])
        right = jnp.concatenate([w1[3 * ab + 1], w1[3 * ab + 2]], axis=0)
        left = jnp.concatenate([zero, w1[3 * ab]], axis=0)
        taps1.append(jnp.concatenate([right, left], axis=1))
    w1_all = jnp.concatenate(taps1, axis=0)

    def vol_rows(plane, b):
        at = 1 if b == 0 else b - 1
        rows = vol_rim[:, at] if plane < 0 else vol[plane, :, at]
        return flat(rows_back(rows) if b == 0 else rows)

    taps_rows = 3 * vol.shape[-1]
    cells = w1.shape[-1]
    height, width = vol.shape[1], vol.shape[3]

    def first_layer(p, planes):
        columns = jnp.concatenate(
            [vol_rows(2 * p + a - 1, b) for a in planes for b in range(3)], axis=1
        )
        return dot(columns, w1_all[planes[0] * taps_rows : (planes[-1] + 1) * taps_rows])

    def activation(both):
        here = both[:, :cells].reshape(height, width, cells)
        left = both[:, cells:].reshape(height, width, cells)
        pre = here + shift_down(left)
        return jnp.where(pre > 0, pre, SLOPE * pre).astype(BF16)

    def keep_hidden(plane, values):
        wide = values.astype(F32)
        hf[plane] = wide.reshape(hf.shape[1:])

    half_h, half_w = hf.shape[1], hf.shape[3] // 2
    even, odd = {}, {}

    def hidden_rows(plane, b, parity):
        at = 1 if b == 0 else b - 1
        rows = hf[plane, :, at, pl.ds(parity, half_w, stride=2), :]
        return flat(rows_back(rows) if b == 0 else rows)

    def second_layer(a):
        taps = range(3 * a, 3 * a + 3)
        for ab in taps:
            even[ab], odd[ab] = hidden_rows(a, ab - 3 * a, 0), hidden_rows(a, ab - 3 * a, 1)
        here = dot(
            jnp.concatenate([x.astype(BF16) for ab in taps for x in (even[ab], odd[ab])], axis=1),
            jnp.concatenate([w2[3 * ab + c] for ab in taps for c in (1, 2)], axis=0),
        )
        left = dot(
            jnp.concatenate([odd[ab].astype(BF16) for ab in taps], axis=1),
            jnp.concatenate([w2[3 * ab] for ab in taps], axis=0),
        )
        for ab in taps:
            even[ab] = jnp.transpose(even[ab]).astype(BF16)
            odd[ab] = jnp.transpose(odd[ab]).astype(BF16)
        return here, left

    hidden = activation(first_layer(1, (0, 1, 2)))
    hidden_send[...] = hidden

    @pl.when(me < spaces - 1)
    def _():
        hidden_copy.start()

    keep_hidden(2, hidden)
    both = first_layer(0, (1, 2))
    here, left = second_layer(2)

    @pl.when(me > 0)
    def _():
        vol_copy.wait_recv()

    @pl.when(first)
    def _():
        vol_rim[...] = jnp.zeros_like(vol_rim)

    keep_hidden(1, activation(both + first_layer(0, (0,))))
    here_1, left_1 = second_layer(1)

    @pl.when(me > 0)
    def _():
        hidden_copy.wait_recv()

    @pl.when(first)
    def _():
        hidden_rim[...] = jnp.zeros_like(hidden_rim)

    keep_hidden(0, hidden_rim[...])
    here_0, left_0 = second_layer(0)
    pre = here + here_1 + here_0
    left = left + left_1 + left_0
    pre = pre + flat(shift_down(left.reshape(half_h, half_w, cells)))
    second_out[...] = jnp.where(pre > 0, pre, SLOPE * pre).astype(BF16)
    g2 = (up[...].astype(F32) * slope_of(pre)).astype(BF16)
    g2_send[...] = g2.reshape(half_h, half_w, cells)

    @pl.when(me > 0)
    def _():
        g2_copy.start()

    g2_wide = g2.astype(F32).reshape(half_h, half_w, cells)
    g2_ahead = shift_up(g2_wide).astype(BF16)
    g2_both = jnp.concatenate([g2, flat(g2_ahead)], axis=1)
    terms2 = []
    for ab in range(9):
        from_odd = dot(odd[ab], g2_both)
        terms2 += [from_odd[:, cells:], dot(even[ab], g2), from_odd[:, :cells]]

    def begin(layer, terms):
        for stream, (stages, tiles, first_tile, of) in zip(streams, plans):
            if of != layer:
                continue
            share = tiles // split_of(stages)
            for tile in range(tiles):
                k = 2 * (first_tile + tile)
                one = terms[k].reshape(groups, GROUP, -1)
                two = jnp.zeros_like(one)
                if k + 1 < len(terms):
                    two = terms[k + 1].reshape(groups, GROUP, -1)
                pair = jnp.concatenate([one, two], axis=1).astype(BF16)
                rows = pl.ds(tile % share * 2 * GROUP, 2 * GROUP)
                for g in range(groups):
                    block = block_index(stages, g, low, tile // share)
                    stream.sums[0][block, rows, :] = pair[g]
            stream.start(0)

    begin(2, terms2)

    @pl.when(me < spaces - 1)
    def _():
        g2_copy.wait_recv()

    @pl.when(last)
    def _():
        g2_next[...] = jnp.zeros_like(g2_next)

    planes = [(g2.reshape(half_h, half_w, cells), g2_ahead)]
    following = g2_next[...]
    planes.append((following, shift_up(following.astype(F32)).astype(BF16)))
    choices = {}
    for plane in range(2):
        for dr in range(2):
            values = planes[plane][dr]
            choices[plane, 0, dr] = flat(values)
            choices[plane, 1, dr] = flat(rows_ahead(values))
    reach = {0: [(1, 0)], 1: [(2, 0), (0, 1)]}
    for u in range(2):
        for v in range(2):
            for w in range(2):
                members = [
                    ((a * 3 + b) * 3 + c, (plane, dq, dr))
                    for a, plane in reach[u]
                    for b, dq in reach[v]
                    for c, dr in reach[w]
                ]
                grad = dot(
                    jnp.concatenate([choices[key] for _, key in members], axis=1),
                    jnp.concatenate([w2[tap] for tap, _ in members], axis=1),
                    ((1,), (1,)),
                )
                grad = grad.astype(BF16).astype(F32).reshape(half_h, half_w, cells)
                at = hf[1 + u, :, v, pl.ds(w, half_w, stride=2), :]
                grad = (grad * slope_of(at)).astype(BF16).astype(F32)
                gf[u, :, v, pl.ds(w, half_w, stride=2), :] = grad

    grad = gf[...].reshape(-1, gf.shape[3], cells)
    grad_t = jnp.concatenate(
        [jnp.transpose(flat(grad)).astype(BF16), jnp.transpose(flat(shift_up(grad))).astype(BF16)],
        axis=0,
    )
    early = [stream for stream, plan in zip(streams, plans) if plan[3] == 2]
    late = [stream for stream, plan in zip(streams, plans) if plan[3] == 1]
    for stream in early:
        stream.finish(0)

    pairs1, lefts1 = [], []
    for a in range(3):
        columns = jnp.concatenate(
            [
                jnp.concatenate([vol_rows(a - 1, b), vol_rows(a + 1, b)], axis=0)
                for b in range(3)
            ],
            axis=1,
        )
        both = dot(grad_t, columns)
        lanes = vol.shape[-1]
        for b in range(3):
            part = both[:, b * lanes : (b + 1) * lanes]
            pairs1.append(part[:cells])
            lefts1.append(part[cells:])
    lane = lax.broadcasted_iota(jnp.int32, lefts1[0].shape, 1)
    half = lanes // 2
    for k in range(0, 9, 2):
        upper = lefts1[k + 1] if k + 1 < 9 else jnp.zeros_like(lefts1[k])
        pairs1.append(jnp.where(lane < half, pltpu.roll(lefts1[k], half, 1), upper))
    begin(1, pairs1)
    for stream in late:
        stream.finish(0)
    for t in range(1, max(len(stream.stages) for stream in streams)):
        for stream in streams:
            if t < len(stream.stages):
                stream.finish(t)

    for ab in range(9):
        centre = sum1[pl.ds(ab * GROUP, GROUP), :]
        side = sum1[pl.ds((9 + ab // 2) * GROUP, GROUP), :]
        if ab % 2:
            side = pltpu.roll(side, half, 1)
        out1[3 * ab] = side[:, :half]
        out1[3 * ab + 1] = centre[:, :half]
        out1[3 * ab + 2] = pltpu.roll(centre, half, 1)[:, :half]

    @pl.when(me < spaces - 1)
    def _():
        vol_copy.wait_send()
        hidden_copy.wait_send()

    @pl.when(me > 0)
    def _():
        g2_copy.wait_send()


def local(volumes, first_filter, second_filter, upstream_grad, spaces, samples):
    _, depth, height, merged = volumes.shape
    c0, c1 = first_filter.shape[3:]
    width = merged // c0
    vol = volumes.reshape(depth, height // 2, 2, width // 2, 2 * c0)
    w1 = first_filter.reshape(27, c0, c1)
    w2 = second_filter.reshape(27, c1, c1)
    _, _, q, r, _ = upstream_grad.shape
    up = upstream_grad.reshape(q * r, c1)
    groups = min(c1 // GROUP, spaces)
    by_space = straight(spaces, samples, groups)
    by_samples = samples_early(spaces, samples, groups) if samples > 1 else by_space
    plans = [(by_space, 6, 0, 2), (by_samples, 8, 6, 2), (by_space, 7, 0, 1)]
    rows2, rows1 = 28 * GROUP, 14 * GROUP

    def buffers(stages, tiles):
        split = split_of(stages)
        rows = tiles * 2 * GROUP // split
        sums, received, size = [], [], groups * split
        for _, _, kind in stages:
            sums.append(pltpu.VMEM((size, rows, c1), BF16))
            size = size // 2 if kind == "halve" else size
            received.append(pltpu.VMEM((size, rows, c1), BF16))
        return sums + received + [pltpu.SemaphoreType.DMA((len(stages),))] * 2

    vmem = pl.BlockSpec(memory_space=pltpu.VMEM)
    second_out, out1, out2 = pl.pallas_call(
        functools.partial(kernel, plans, spaces, groups),
        out_shape=(
            jax.ShapeDtypeStruct((q * r, c1), BF16),
            jax.ShapeDtypeStruct((27, GROUP, c0), F32),
            jax.ShapeDtypeStruct((rows2, c1), F32),
        ),
        in_specs=[vmem] * 4,
        out_specs=(vmem,) * 3,
        scratch_shapes=[
            pltpu.VMEM((height // 2, 2, width // 2, 2 * c0), BF16),
            pltpu.VMEM((height // 2, width // 2, c1), BF16),
            pltpu.VMEM((height // 2, width // 2, c1), BF16),
            pltpu.VMEM((3, height // 4, 2, width // 2, c1), F32),
            pltpu.VMEM((q, r, c1), BF16),
            pltpu.VMEM((q, r, c1), BF16),
            pltpu.VMEM((2, height // 4, 2, width // 2, c1), F32),
            pltpu.VMEM((rows1, c1), F32),
            pltpu.SemaphoreType.DMA((3,)),
            pltpu.SemaphoreType.DMA((3,)),
            *[each for plan in plans for each in buffers(*plan[:2])],
        ],
        compiler_params=pltpu.CompilerParams(
            collective_id=0, has_side_effects=True, vmem_limit_bytes=50 * 1024 * 1024
        ),
    )(vol, w1, w2, up)

    own = c1 // spaces
    start = (lax.axis_index("space") % (GROUP // own)) * own if own < GROUP else 0
    units2 = out2.reshape(28, GROUP, c1)[:27]
    if own < GROUP:
        units2 = lax.dynamic_slice_in_dim(units2, start, own, 1)
        out1 = lax.dynamic_slice_in_dim(out1, start, own, 1)
    second_grad = units2.reshape(3, 3, 3, own, c1)
    first_grad = jnp.transpose(out1.reshape(3, 3, 3, own, c0), (0, 1, 2, 4, 3))
    return second_out.reshape(1, 1, q, r, c1), first_grad, second_grad


def solution(mesh):
    placed = (P("dp", "space", None, None), P(), P(), P("dp", "space", None, None, None))
    body = functools.partial(local, spaces=mesh.shape["space"], samples=mesh.shape["dp"])
    return jax.shard_map(
        body,
        mesh=mesh,
        in_specs=placed,
        out_specs=(
            P("dp", "space", None, None, None),
            P(None, None, None, None, "space"),
            P(None, None, None, "space", None),
        ),
        check_vma=False,
    )
```

```python
import functools

import jax
import jax.numpy as jnp
from jax import lax
from jax.experimental import pallas as pl
from jax.experimental.pallas import tpu as pltpu
from jax.sharding import PartitionSpec as P

SLOPE = 0.3
F32, BF16 = jnp.float32, jnp.bfloat16
MESH = pl.DeviceIdType.MESH
GROUP = 8


def dot(lhs, rhs, contract=((1,), (0,))):
    return lax.dot_general(lhs, rhs, (contract, ((), ())), preferred_element_type=F32)


def log2(n):
    return n.bit_length() - 1


def bits_of(spaces, groups):
    extra = log2(spaces) - log2(groups)
    return list(range(extra, log2(spaces))), list(range(extra))


def straight(spaces, samples, groups, crossed=False):
    halving, shared = bits_of(spaces, groups)
    if crossed:
        halving = halving[:1] + halving[2:3] + halving[1:2] + halving[3:]
    stages = [("space", k, "halve") for k in halving]
    stages += [("space", k, "full") for k in shared]
    return stages + [("dp", k, "full") for k in range(log2(samples))]


def samples_early(spaces, samples, groups):
    halving, shared = bits_of(spaces, groups)
    stages = [("space", k, "halve") for k in halving]
    stages.insert(1, ("dp", 0, "halve"))
    stages += [("space", k, "full") for k in shared]
    stages += [("dp", k, "full") for k in range(1, log2(samples))]
    return stages + [("dp", 0, "gather")]


def block_index(stages, group, low, sample_half):
    index = 0
    for axis, bit, kind in stages:
        if kind == "halve":
            value = (group >> (bit - low)) & 1 if axis == "space" else sample_half
            index = 2 * index + value
    return index


def split_of(stages):
    return 2 if stages[-1][2] == "gather" else 1


def shift_down(values, axis=1):
    at = lax.broadcasted_iota(jnp.int32, values.shape, axis)
    return jnp.where(at == 0, 0.0, pltpu.roll(values, 1, axis))


def shift_up(values, axis=1):
    size = values.shape[axis]
    at = lax.broadcasted_iota(jnp.int32, values.shape, axis)
    return jnp.where(at == size - 1, 0.0, pltpu.roll(values, size - 1, axis))


def rows_back(values):
    return jnp.concatenate([jnp.zeros_like(values[:1]), values[:-1]], axis=0)


def rows_ahead(values):
    return jnp.concatenate([values[1:], jnp.zeros_like(values[:1])], axis=0)


def flat(values):
    return values.reshape(-1, values.shape[-1])


def slope_of(values):
    return jnp.where(values > 0, 1.0, SLOPE)


class Reduction:
    def __init__(self, stages, scratch, out, out_row):
        count = len(stages)
        self.stages, self.out, self.out_row = stages, out, out_row
        self.sums, self.received = scratch[:count], scratch[count : 2 * count]
        self.sends, self.receives = scratch[2 * count :]
        self.copy = None

    def start(self, t):
        axis, bit, kind = self.stages[t]
        me = lax.axis_index(axis)
        own = (me // (1 << bit)) % 2
        partner = me + (1 - 2 * own) * (1 << bit)
        held = self.sums[t]
        source = held
        if kind == "halve":
            half = held.shape[0] // 2
            source = held.at[pl.ds((1 - own) * half, half)]
        self.copy = pltpu.make_async_remote_copy(
            src_ref=source,
            dst_ref=self.received[t],
            send_sem=self.sends.at[t],
            recv_sem=self.receives.at[t],
            device_id={axis: partner},
            device_id_type=MESH,
        )
        self.copy.start()
        self.own = own

    def finish(self, t):
        self.copy.wait()
        kind = self.stages[t][2]
        held = self.sums[t]
        rows = held.shape[1]
        if kind == "gather":
            for half, values in ((self.own, held), (1 - self.own, self.received[t])):
                at = pl.multiple_of(self.out_row + half * rows, GROUP)
                self.out[pl.ds(at, rows), :] = values[0].astype(F32)
            return
        if kind == "halve":
            half = held.shape[0] // 2
            mine = held[pl.ds(self.own * half, half)]
        else:
            mine = held[...]
        total = mine.astype(F32) + self.received[t][...].astype(F32)
        if t + 1 < len(self.stages):
            self.sums[t + 1][...] = total.astype(BF16)
            self.start(t + 1)
        else:
            self.out[pl.ds(self.out_row, rows), :] = total[0]


def kernel(plans, spaces, groups, vol, w1, w2, up, second_out, out1, out2, *scratch):
    (vol_rim, hidden_send, hidden_rim, hf, g2_send, g2_next, gf, sum1, halo_send, halo_recv) = scratch[:10]
    at, streams = 10, []
    for stages, tiles, first_tile, layer in plans:
        used = 2 * len(stages) + 2
        target = out2 if layer == 2 else sum1
        streams.append(Reduction(stages, scratch[at : at + used], target, first_tile * 2 * GROUP))
        at += used
    low = log2(spaces) - log2(groups)
    me = lax.axis_index("space")
    first, last = me == 0, me == spaces - 1

    barrier = pltpu.get_barrier_semaphore()
    partners = sorted({stage[:2] for plan in plans for stage in plan[0]})
    for axis, bit in partners:
        at = lax.axis_index(axis)
        partner = at + (1 - 2 * ((at // (1 << bit)) % 2)) * (1 << bit)
        pl.semaphore_signal(barrier, inc=1, device_id={axis: partner}, device_id_type=MESH)

    @pl.when(me > 0)
    def _():
        pl.semaphore_signal(barrier, inc=1, device_id={"space": me - 1}, device_id_type=MESH)

    @pl.when(me < spaces - 1)
    def _():
        pl.semaphore_signal(barrier, inc=1, device_id={"space": me + 1}, device_id_type=MESH)

    ends = jnp.where(first, 1, 0) + jnp.where(last, 1, 0)
    pl.semaphore_wait(barrier, len(partners) + 2 - ends)

    def halo(index, source, target, by):
        return pltpu.make_async_remote_copy(
            src_ref=source,
            dst_ref=target,
            send_sem=halo_send.at[index],
            recv_sem=halo_recv.at[index],
            device_id={"space": me + by},
            device_id_type=MESH,
        )

    vol_copy = halo(0, vol.at[vol.shape[0] - 1], vol_rim, 1)
    hidden_copy = halo(1, hidden_send, hidden_rim, 1)
    g2_copy = halo(2, g2_send, g2_next, -1)

    @pl.when(me < spaces - 1)
    def _():
        vol_copy.start()

    taps1 = []
    for ab in range(9):
        zero = jnp.zeros_like(w1[0])
        right = jnp.concatenate([w1[3 * ab + 1], w1[3 * ab + 2]], axis=0)
        left = jnp.concatenate([zero, w1[3 * ab]], axis=0)
        taps1.append(jnp.concatenate([right, left], axis=1))
    w1_all = jnp.concatenate(taps1, axis=0)

    def vol_rows(plane, b):
        at = 1 if b == 0 else b - 1
        rows = vol_rim[:, at] if plane < 0 else vol[plane, :, at]
        return flat(rows_back(rows) if b == 0 else rows)

    taps_rows = 3 * vol.shape[-1]
    cells = w1.shape[-1]
    height, width = vol.shape[1], vol.shape[3]

    def first_layer(p, planes):
        columns = jnp.concatenate(
            [vol_rows(2 * p + a - 1, b) for a in planes for b in range(3)], axis=1
        )
        return dot(columns, w1_all[planes[0] * taps_rows : (planes[-1] + 1) * taps_rows])

    def activation(both):
        here = both[:, :cells].reshape(height, width, cells)
        left = both[:, cells:].reshape(height, width, cells)
        pre = here + shift_down(left)
        return jnp.where(pre > 0, pre, SLOPE * pre).astype(BF16)

    def keep_hidden(plane, values):
        wide = values.astype(F32)
        hf[plane] = wide.reshape(hf.shape[1:])

    half_h, half_w = hf.shape[1], hf.shape[3] // 2
    even, odd = {}, {}

    def hidden_rows(plane, b, parity):
        at = 1 if b == 0 else b - 1
        rows = hf[plane, :, at, pl.ds(parity, half_w, stride=2), :]
        return flat(rows_back(rows) if b == 0 else rows)

    def second_layer(a):
        taps = range(3 * a, 3 * a + 3)
        for ab in taps:
            even[ab], odd[ab] = hidden_rows(a, ab - 3 * a, 0), hidden_rows(a, ab - 3 * a, 1)
        here = dot(
            jnp.concatenate([x.astype(BF16) for ab in taps for x in (even[ab], odd[ab])], axis=1),
            jnp.concatenate([w2[3 * ab + c] for ab in taps for c in (1, 2)], axis=0),
        )
        left = dot(
            jnp.concatenate([odd[ab].astype(BF16) for ab in taps], axis=1),
            jnp.concatenate([w2[3 * ab] for ab in taps], axis=0),
        )
        for ab in taps:
            even[ab] = jnp.transpose(even[ab]).astype(BF16)
            odd[ab] = jnp.transpose(odd[ab]).astype(BF16)
        return here, left

    hidden = activation(first_layer(1, (0, 1, 2)))
    hidden_send[...] = hidden

    @pl.when(me < spaces - 1)
    def _():
        hidden_copy.start()

    keep_hidden(2, hidden)
    both = first_layer(0, (1, 2))
    here, left = second_layer(2)

    @pl.when(me > 0)
    def _():
        vol_copy.wait_recv()

    @pl.when(first)
    def _():
        vol_rim[...] = jnp.zeros_like(vol_rim)

    keep_hidden(1, activation(both + first_layer(0, (0,))))
    here_1, left_1 = second_layer(1)

    @pl.when(me > 0)
    def _():
        hidden_copy.wait_recv()

    @pl.when(first)
    def _():
        hidden_rim[...] = jnp.zeros_like(hidden_rim)

    keep_hidden(0, hidden_rim[...])
    here_0, left_0 = second_layer(0)
    pre = here + here_1 + here_0
    left = left + left_1 + left_0
    pre = pre + flat(shift_down(left.reshape(half_h, half_w, cells)))
    second_out[...] = jnp.where(pre > 0, pre, SLOPE * pre).astype(BF16)
    g2 = (up[...].astype(F32) * slope_of(pre)).astype(BF16)
    g2_send[...] = g2.reshape(half_h, half_w, cells)

    @pl.when(me > 0)
    def _():
        g2_copy.start()

    g2_wide = g2.astype(F32).reshape(half_h, half_w, cells)
    g2_ahead = shift_up(g2_wide).astype(BF16)
    g2_both = jnp.concatenate([g2, flat(g2_ahead)], axis=1)
    terms2 = []
    for ab in range(9):
        from_odd = dot(odd[ab], g2_both)
        terms2 += [from_odd[:, cells:], dot(even[ab], g2), from_odd[:, :cells]]

    def begin(layer, terms):
        for stream, (stages, tiles, first_tile, of) in zip(streams, plans):
            if of != layer:
                continue
            share = tiles // split_of(stages)
            for tile in range(tiles):
                k = 2 * (first_tile + tile)
                one = terms[k].reshape(groups, GROUP, -1)
                two = jnp.zeros_like(one)
                if k + 1 < len(terms):
                    two = terms[k + 1].reshape(groups, GROUP, -1)
                pair = jnp.concatenate([one, two], axis=1).astype(BF16)
                rows = pl.ds(tile % share * 2 * GROUP, 2 * GROUP)
                for g in range(groups):
                    block = block_index(stages, g, low, tile // share)
                    stream.sums[0][block, rows, :] = pair[g]
            stream.start(0)

    begin(2, terms2)

    @pl.when(me < spaces - 1)
    def _():
        g2_copy.wait_recv()

    @pl.when(last)
    def _():
        g2_next[...] = jnp.zeros_like(g2_next)

    planes = [(g2.reshape(half_h, half_w, cells), g2_ahead)]
    following = g2_next[...]
    planes.append((following, shift_up(following.astype(F32)).astype(BF16)))
    choices = {}
    for plane in range(2):
        for dr in range(2):
            values = planes[plane][dr]
            choices[plane, 0, dr] = flat(values)
            choices[plane, 1, dr] = flat(rows_ahead(values))
    reach = {0: [(1, 0)], 1: [(2, 0), (0, 1)]}
    for u in range(2):
        for v in range(2):
            for w in range(2):
                members = [
                    ((a * 3 + b) * 3 + c, (plane, dq, dr))
                    for a, plane in reach[u]
                    for b, dq in reach[v]
                    for c, dr in reach[w]
                ]
                grad = dot(
                    jnp.concatenate([choices[key] for _, key in members], axis=1),
                    jnp.concatenate([w2[tap] for tap, _ in members], axis=1),
                    ((1,), (1,)),
                )
                grad = grad.astype(BF16).astype(F32).reshape(half_h, half_w, cells)
                at = hf[1 + u, :, v, pl.ds(w, half_w, stride=2), :]
                grad = (grad * slope_of(at)).astype(BF16).astype(F32)
                gf[u, :, v, pl.ds(w, half_w, stride=2), :] = grad

    early = [stream for stream, plan in zip(streams, plans) if plan[3] == 2]
    late = [stream for stream, plan in zip(streams, plans) if plan[3] == 1]
    for stream in early:
        stream.finish(0)

    grad = gf[...].reshape(-1, gf.shape[3], cells)
    grad_t = jnp.concatenate(
        [jnp.transpose(flat(grad)).astype(BF16), jnp.transpose(flat(shift_up(grad))).astype(BF16)],
        axis=0,
    )
    pairs1, lefts1 = [], []
    for a in range(3):
        columns = jnp.concatenate(
            [
                jnp.concatenate([vol_rows(a - 1, b), vol_rows(a + 1, b)], axis=0)
                for b in range(3)
            ],
            axis=1,
        )
        both = dot(grad_t, columns)
        lanes = vol.shape[-1]
        for b in range(3):
            part = both[:, b * lanes : (b + 1) * lanes]
            pairs1.append(part[:cells])
            lefts1.append(part[cells:])
    lane = lax.broadcasted_iota(jnp.int32, lefts1[0].shape, 1)
    half = lanes // 2
    for k in range(0, 9, 2):
        upper = lefts1[k + 1] if k + 1 < 9 else jnp.zeros_like(lefts1[k])
        pairs1.append(jnp.where(lane < half, pltpu.roll(lefts1[k], half, 1), upper))
    begin(1, pairs1)
    for stream in late:
        stream.finish(0)
    for t in range(1, max(len(stream.stages) for stream in streams) + 1):
        for stream in early:
            if t < len(stream.stages):
                stream.finish(t)
        for stream in late:
            if 1 < t <= len(stream.stages):
                stream.finish(t - 1)

    for ab in range(9):
        centre = sum1[pl.ds(ab * GROUP, GROUP), :]
        side = sum1[pl.ds((9 + ab // 2) * GROUP, GROUP), :]
        if ab % 2:
            side = pltpu.roll(side, half, 1)
        out1[3 * ab] = side[:, :half]
        out1[3 * ab + 1] = centre[:, :half]
        out1[3 * ab + 2] = pltpu.roll(centre, half, 1)[:, :half]

    @pl.when(me < spaces - 1)
    def _():
        vol_copy.wait_send()
        hidden_copy.wait_send()

    @pl.when(me > 0)
    def _():
        g2_copy.wait_send()


def local(volumes, first_filter, second_filter, upstream_grad, spaces, samples):
    _, depth, height, merged = volumes.shape
    c0, c1 = first_filter.shape[3:]
    width = merged // c0
    vol = volumes.reshape(depth, height // 2, 2, width // 2, 2 * c0)
    w1 = first_filter.reshape(27, c0, c1)
    w2 = second_filter.reshape(27, c1, c1)
    _, _, q, r, _ = upstream_grad.shape
    up = upstream_grad.reshape(q * r, c1)
    groups = min(c1 // GROUP, spaces)
    by_space = straight(spaces, samples, groups)
    by_samples = samples_early(spaces, samples, groups) if samples > 1 else by_space
    crossed = straight(spaces, samples, groups, True)
    plans = [(by_space, 6, 0, 2), (by_samples, 8, 6, 2), (by_space, 4, 0, 1), (crossed, 3, 4, 1)]
    rows2, rows1 = 28 * GROUP, 14 * GROUP

    def buffers(stages, tiles):
        split = split_of(stages)
        rows = tiles * 2 * GROUP // split
        sums, received, size = [], [], groups * split
        for _, _, kind in stages:
            sums.append(pltpu.VMEM((size, rows, c1), BF16))
            size = size // 2 if kind == "halve" else size
            received.append(pltpu.VMEM((size, rows, c1), BF16))
        return sums + received + [pltpu.SemaphoreType.DMA((len(stages),))] * 2

    vmem = pl.BlockSpec(memory_space=pltpu.VMEM)
    second_out, out1, out2 = pl.pallas_call(
        functools.partial(kernel, plans, spaces, groups),
        out_shape=(
            jax.ShapeDtypeStruct((q * r, c1), BF16),
            jax.ShapeDtypeStruct((27, GROUP, c0), F32),
            jax.ShapeDtypeStruct((rows2, c1), F32),
        ),
        in_specs=[vmem] * 4,
        out_specs=(vmem,) * 3,
        scratch_shapes=[
            pltpu.VMEM((height // 2, 2, width // 2, 2 * c0), BF16),
            pltpu.VMEM((height // 2, width // 2, c1), BF16),
            pltpu.VMEM((height // 2, width // 2, c1), BF16),
            pltpu.VMEM((3, height // 4, 2, width // 2, c1), F32),
            pltpu.VMEM((q, r, c1), BF16),
            pltpu.VMEM((q, r, c1), BF16),
            pltpu.VMEM((2, height // 4, 2, width // 2, c1), F32),
            pltpu.VMEM((rows1, c1), F32),
            pltpu.SemaphoreType.DMA((3,)),
            pltpu.SemaphoreType.DMA((3,)),
            *[each for plan in plans for each in buffers(*plan[:2])],
        ],
        compiler_params=pltpu.CompilerParams(
            collective_id=0, has_side_effects=True, vmem_limit_bytes=50 * 1024 * 1024
        ),
    )(vol, w1, w2, up)

    own = c1 // spaces
    start = (lax.axis_index("space") % (GROUP // own)) * own if own < GROUP else 0
    units2 = out2.reshape(28, GROUP, c1)[:27]
    if own < GROUP:
        units2 = lax.dynamic_slice_in_dim(units2, start, own, 1)
        out1 = lax.dynamic_slice_in_dim(out1, start, own, 1)
    second_grad = units2.reshape(3, 3, 3, own, c1)
    first_grad = jnp.transpose(out1.reshape(3, 3, 3, own, c0), (0, 1, 2, 4, 3))
    return second_out.reshape(1, 1, q, r, c1), first_grad, second_grad


def solution(mesh):
    placed = (P("dp", "space", None, None), P(), P(), P("dp", "space", None, None, None))
    body = functools.partial(local, spaces=mesh.shape["space"], samples=mesh.shape["dp"])
    return jax.shard_map(
        body,
        mesh=mesh,
        in_specs=placed,
        out_specs=(
            P("dp", "space", None, None, None),
            P(None, None, None, None, "space"),
            P(None, None, None, "space", None),
        ),
        check_vma=False,
    )
```

```python
import functools

import jax
import jax.numpy as jnp
from jax import lax
from jax.experimental import pallas as pl
from jax.experimental.pallas import tpu as pltpu
from jax.sharding import PartitionSpec as P

SLOPE = 0.3
F32, BF16 = jnp.float32, jnp.bfloat16
MESH = pl.DeviceIdType.MESH
GROUP = 8


def dot(lhs, rhs, contract=((1,), (0,))):
    return lax.dot_general(lhs, rhs, (contract, ((), ())), preferred_element_type=F32)


def log2(n):
    return n.bit_length() - 1


def bits_of(spaces, groups):
    extra = log2(spaces) - log2(groups)
    return list(range(extra, log2(spaces))), list(range(extra))


def straight(spaces, samples, groups, crossed=False):
    halving, shared = bits_of(spaces, groups)
    if crossed:
        halving = halving[:1] + halving[2:3] + halving[1:2] + halving[3:]
    stages = [("space", k, "halve") for k in halving]
    stages += [("space", k, "full") for k in shared]
    return stages + [("dp", k, "full") for k in range(log2(samples))]


def samples_early(spaces, samples, groups):
    halving, shared = bits_of(spaces, groups)
    stages = [("space", k, "halve") for k in halving]
    stages.insert(1, ("dp", 0, "halve"))
    stages += [("space", k, "full") for k in shared]
    stages += [("dp", k, "full") for k in range(1, log2(samples))]
    return stages + [("dp", 0, "gather")]


def block_index(stages, group, low, sample_half):
    index = 0
    for axis, bit, kind in stages:
        if kind == "halve":
            value = (group >> (bit - low)) & 1 if axis == "space" else sample_half
            index = 2 * index + value
    return index


def split_of(stages):
    return 2 if stages[-1][2] == "gather" else 1


def shift_down(values, axis=1):
    at = lax.broadcasted_iota(jnp.int32, values.shape, axis)
    return jnp.where(at == 0, 0.0, pltpu.roll(values, 1, axis))


def shift_up(values, axis=1):
    size = values.shape[axis]
    at = lax.broadcasted_iota(jnp.int32, values.shape, axis)
    return jnp.where(at == size - 1, 0.0, pltpu.roll(values, size - 1, axis))


def rows_back(values):
    return jnp.concatenate([jnp.zeros_like(values[:1]), values[:-1]], axis=0)


def rows_ahead(values):
    return jnp.concatenate([values[1:], jnp.zeros_like(values[:1])], axis=0)


def flat(values):
    return values.reshape(-1, values.shape[-1])


def slope_of(values):
    return jnp.where(values > 0, 1.0, SLOPE)


class Reduction:
    def __init__(self, stages, scratch, out, out_row):
        count = len(stages)
        self.stages, self.out, self.out_row = stages, out, out_row
        self.sums, self.received = scratch[:count], scratch[count : 2 * count]
        self.sends, self.receives = scratch[2 * count :]
        self.copy = None

    def start(self, t):
        axis, bit, kind = self.stages[t]
        me = lax.axis_index(axis)
        own = (me // (1 << bit)) % 2
        partner = me + (1 - 2 * own) * (1 << bit)
        held = self.sums[t]
        source = held
        if kind == "halve":
            half = held.shape[0] // 2
            source = held.at[pl.ds((1 - own) * half, half)]
        self.copy = pltpu.make_async_remote_copy(
            src_ref=source,
            dst_ref=self.received[t],
            send_sem=self.sends.at[t],
            recv_sem=self.receives.at[t],
            device_id={axis: partner},
            device_id_type=MESH,
        )
        self.copy.start()
        self.own = own

    def finish(self, t):
        self.copy.wait()
        kind = self.stages[t][2]
        held = self.sums[t]
        rows = held.shape[1]
        if kind == "gather":
            for half, values in ((self.own, held), (1 - self.own, self.received[t])):
                at = pl.multiple_of(self.out_row + half * rows, GROUP)
                self.out[pl.ds(at, rows), :] = values[0].astype(F32)
            return
        if kind == "halve":
            half = held.shape[0] // 2
            mine = held[pl.ds(self.own * half, half)]
        else:
            mine = held[...]
        total = mine.astype(F32) + self.received[t][...].astype(F32)
        if t + 1 < len(self.stages):
            self.sums[t + 1][...] = total.astype(BF16)
            self.start(t + 1)
        else:
            self.out[pl.ds(self.out_row, rows), :] = total[0]


def kernel(plans, spaces, groups, vol, w1, w2, up, second_out, out1, out2, *scratch):
    (vol_rim, hidden_send, hidden_rim, hf, g2_send, g2_next, gf, sum1, sum2, halo_send, halo_recv) = scratch[:11]
    at, streams = 11, []
    for stages, tiles, first_tile, layer in plans:
        used = 2 * len(stages) + 2
        target = sum2 if layer == 2 else sum1
        streams.append(Reduction(stages, scratch[at : at + used], target, first_tile * 2 * GROUP))
        at += used
    low = log2(spaces) - log2(groups)
    me = lax.axis_index("space")
    first, last = me == 0, me == spaces - 1

    barrier = pltpu.get_barrier_semaphore()
    partners = sorted({stage[:2] for plan in plans for stage in plan[0]})
    for axis, bit in partners:
        at = lax.axis_index(axis)
        partner = at + (1 - 2 * ((at // (1 << bit)) % 2)) * (1 << bit)
        pl.semaphore_signal(barrier, inc=1, device_id={axis: partner}, device_id_type=MESH)

    @pl.when(me > 0)
    def _():
        pl.semaphore_signal(barrier, inc=1, device_id={"space": me - 1}, device_id_type=MESH)

    @pl.when(me < spaces - 1)
    def _():
        pl.semaphore_signal(barrier, inc=1, device_id={"space": me + 1}, device_id_type=MESH)

    ends = jnp.where(first, 1, 0) + jnp.where(last, 1, 0)
    pl.semaphore_wait(barrier, len(partners) + 2 - ends)

    def halo(index, source, target, by):
        return pltpu.make_async_remote_copy(
            src_ref=source,
            dst_ref=target,
            send_sem=halo_send.at[index],
            recv_sem=halo_recv.at[index],
            device_id={"space": me + by},
            device_id_type=MESH,
        )

    vol_copy = halo(0, vol.at[vol.shape[0] - 1], vol_rim, 1)
    hidden_copy = halo(1, hidden_send, hidden_rim, 1)
    g2_copy = halo(2, g2_send, g2_next, -1)

    @pl.when(me < spaces - 1)
    def _():
        vol_copy.start()

    taps1 = []
    for ab in range(9):
        zero = jnp.zeros_like(w1[0])
        right = jnp.concatenate([w1[3 * ab + 1], w1[3 * ab + 2]], axis=0)
        left = jnp.concatenate([zero, w1[3 * ab]], axis=0)
        taps1.append(jnp.concatenate([right, left], axis=1))
    w1_all = jnp.concatenate(taps1, axis=0)

    def vol_rows(plane, b):
        at = 1 if b == 0 else b - 1
        rows = vol_rim[:, at] if plane < 0 else vol[plane, :, at]
        return flat(rows_back(rows) if b == 0 else rows)

    taps_rows = 3 * vol.shape[-1]
    cells = w1.shape[-1]
    height, width = vol.shape[1], vol.shape[3]

    def first_layer(p, planes):
        columns = jnp.concatenate(
            [vol_rows(2 * p + a - 1, b) for a in planes for b in range(3)], axis=1
        )
        return dot(columns, w1_all[planes[0] * taps_rows : (planes[-1] + 1) * taps_rows])

    def activation(both):
        here = both[:, :cells].reshape(height, width, cells)
        left = both[:, cells:].reshape(height, width, cells)
        pre = here + shift_down(left)
        return jnp.where(pre > 0, pre, SLOPE * pre).astype(BF16)

    def keep_hidden(plane, values):
        wide = values.astype(F32)
        hf[plane] = wide.reshape(hf.shape[1:])

    half_h, half_w = hf.shape[1], hf.shape[3] // 2
    even, odd = {}, {}

    def hidden_rows(plane, b, parity):
        at = 1 if b == 0 else b - 1
        rows = hf[plane, :, at, pl.ds(parity, half_w, stride=2), :]
        return flat(rows_back(rows) if b == 0 else rows)

    def second_layer(a):
        taps = range(3 * a, 3 * a + 3)
        for ab in taps:
            even[ab], odd[ab] = hidden_rows(a, ab - 3 * a, 0), hidden_rows(a, ab - 3 * a, 1)
        here = dot(
            jnp.concatenate([x.astype(BF16) for ab in taps for x in (even[ab], odd[ab])], axis=1),
            jnp.concatenate([w2[3 * ab + c] for ab in taps for c in (1, 2)], axis=0),
        )
        left = dot(
            jnp.concatenate([odd[ab].astype(BF16) for ab in taps], axis=1),
            jnp.concatenate([w2[3 * ab] for ab in taps], axis=0),
        )
        for ab in taps:
            even[ab] = jnp.transpose(even[ab]).astype(BF16)
            odd[ab] = jnp.transpose(odd[ab]).astype(BF16)
        return here, left

    hidden = activation(first_layer(1, (0, 1, 2)))
    hidden_send[...] = hidden

    @pl.when(me < spaces - 1)
    def _():
        hidden_copy.start()

    keep_hidden(2, hidden)
    both = first_layer(0, (1, 2))
    here, left = second_layer(2)

    @pl.when(me > 0)
    def _():
        vol_copy.wait_recv()

    @pl.when(first)
    def _():
        vol_rim[...] = jnp.zeros_like(vol_rim)

    keep_hidden(1, activation(both + first_layer(0, (0,))))
    here_1, left_1 = second_layer(1)

    @pl.when(me > 0)
    def _():
        hidden_copy.wait_recv()

    @pl.when(first)
    def _():
        hidden_rim[...] = jnp.zeros_like(hidden_rim)

    keep_hidden(0, hidden_rim[...])
    here_0, left_0 = second_layer(0)
    pre = here + here_1 + here_0
    left = left + left_1 + left_0
    pre = pre + flat(shift_down(left.reshape(half_h, half_w, cells)))
    second_out[...] = jnp.where(pre > 0, pre, SLOPE * pre).astype(BF16)
    g2 = (up[...].astype(F32) * slope_of(pre)).astype(BF16)
    g2_send[...] = g2.reshape(half_h, half_w, cells)

    @pl.when(me > 0)
    def _():
        g2_copy.start()

    g2_wide = g2.astype(F32).reshape(half_h, half_w, cells)
    g2_ahead = shift_up(g2_wide).astype(BF16)
    g2_both = jnp.concatenate([g2, flat(g2_ahead)], axis=1)
    terms2 = []
    for ab in range(9):
        from_odd = dot(odd[ab], g2_both)
        terms2 += [from_odd[:, cells:], dot(even[ab], g2), from_odd[:, :cells]]

    def begin(layer, terms):
        for stream, (stages, tiles, first_tile, of) in zip(streams, plans):
            if of != layer:
                continue
            share = tiles // split_of(stages)
            for tile in range(tiles):
                k = 2 * (first_tile + tile)
                one = terms[k].reshape(groups, GROUP, -1)
                two = jnp.zeros_like(one)
                if k + 1 < len(terms):
                    two = terms[k + 1].reshape(groups, GROUP, -1)
                pair = jnp.concatenate([one, two], axis=1).astype(BF16)
                rows = pl.ds(tile % share * 2 * GROUP, 2 * GROUP)
                for g in range(groups):
                    block = block_index(stages, g, low, tile // share)
                    stream.sums[0][block, rows, :] = pair[g]
            stream.start(0)

    begin(2, terms2)

    @pl.when(me < spaces - 1)
    def _():
        g2_copy.wait_recv()

    @pl.when(last)
    def _():
        g2_next[...] = jnp.zeros_like(g2_next)

    planes = [(g2.reshape(half_h, half_w, cells), g2_ahead)]
    following = g2_next[...]
    planes.append((following, shift_up(following.astype(F32)).astype(BF16)))
    choices = {}
    for plane in range(2):
        for dr in range(2):
            values = planes[plane][dr]
            choices[plane, 0, dr] = flat(values)
            choices[plane, 1, dr] = flat(rows_ahead(values))
    reach = {0: [(1, 0)], 1: [(2, 0), (0, 1)]}
    for u in range(2):
        for v in range(2):
            for w in range(2):
                members = [
                    ((a * 3 + b) * 3 + c, (plane, dq, dr))
                    for a, plane in reach[u]
                    for b, dq in reach[v]
                    for c, dr in reach[w]
                ]
                grad = dot(
                    jnp.concatenate([choices[key] for _, key in members], axis=1),
                    jnp.concatenate([w2[tap] for tap, _ in members], axis=1),
                    ((1,), (1,)),
                )
                grad = grad.astype(BF16).astype(F32).reshape(half_h, half_w, cells)
                at = hf[1 + u, :, v, pl.ds(w, half_w, stride=2), :]
                grad = (grad * slope_of(at)).astype(BF16).astype(F32)
                gf[u, :, v, pl.ds(w, half_w, stride=2), :] = grad

    early = [stream for stream, plan in zip(streams, plans) if plan[3] == 2]
    late = [stream for stream, plan in zip(streams, plans) if plan[3] == 1]
    for stream in early:
        stream.finish(0)

    grad = gf[...].reshape(-1, gf.shape[3], cells)
    grad_t = jnp.concatenate(
        [jnp.transpose(flat(grad)).astype(BF16), jnp.transpose(flat(shift_up(grad))).astype(BF16)],
        axis=0,
    )
    pairs1, lefts1 = [], []
    for a in range(3):
        columns = jnp.concatenate(
            [
                jnp.concatenate([vol_rows(a - 1, b), vol_rows(a + 1, b)], axis=0)
                for b in range(3)
            ],
            axis=1,
        )
        both = dot(grad_t, columns)
        lanes = vol.shape[-1]
        for b in range(3):
            part = both[:, b * lanes : (b + 1) * lanes]
            pairs1.append(part[:cells])
            lefts1.append(part[cells:])
    lane = lax.broadcasted_iota(jnp.int32, lefts1[0].shape, 1)
    half = lanes // 2
    for k in range(0, 9, 2):
        upper = lefts1[k + 1] if k + 1 < 9 else jnp.zeros_like(lefts1[k])
        pairs1.append(jnp.where(lane < half, pltpu.roll(lefts1[k], half, 1), upper))
    begin(1, pairs1)
    for stream in late:
        stream.finish(0)
    for t in range(1, max(len(stream.stages) for stream in streams) + 1):
        for stream in early:
            if t < len(stream.stages):
                stream.finish(t)
        for stream in late:
            if 1 < t <= len(stream.stages):
                stream.finish(t - 1)

    out2[...] = sum2[pl.ds(0, out2.shape[0]), :]
    for ab in range(9):
        centre = sum1[pl.ds(ab * GROUP, GROUP), :]
        side = sum1[pl.ds((9 + ab // 2) * GROUP, GROUP), :]
        if ab % 2:
            side = pltpu.roll(side, half, 1)
        out1[3 * ab] = side[:, :half]
        out1[3 * ab + 1] = centre[:, :half]
        out1[3 * ab + 2] = pltpu.roll(centre, half, 1)[:, :half]

    @pl.when(me < spaces - 1)
    def _():
        vol_copy.wait_send()
        hidden_copy.wait_send()

    @pl.when(me > 0)
    def _():
        g2_copy.wait_send()


def local(volumes, first_filter, second_filter, upstream_grad, spaces, samples):
    _, depth, height, merged = volumes.shape
    c0, c1 = first_filter.shape[3:]
    width = merged // c0
    vol = volumes.reshape(depth, height // 2, 2, width // 2, 2 * c0)
    w1 = first_filter.reshape(27, c0, c1)
    w2 = second_filter.reshape(27, c1, c1)
    _, _, q, r, _ = upstream_grad.shape
    up = upstream_grad.reshape(q * r, c1)
    groups = min(c1 // GROUP, spaces)
    by_space = straight(spaces, samples, groups)
    by_samples = samples_early(spaces, samples, groups) if samples > 1 else by_space
    crossed = straight(spaces, samples, groups, True)
    plans = [(by_space, 6, 0, 2), (by_samples, 8, 6, 2), (by_space, 4, 0, 1), (crossed, 3, 4, 1)]
    rows2, rows1 = 28 * GROUP, 14 * GROUP

    def buffers(stages, tiles):
        split = split_of(stages)
        rows = tiles * 2 * GROUP // split
        sums, received, size = [], [], groups * split
        for _, _, kind in stages:
            sums.append(pltpu.VMEM((size, rows, c1), BF16))
            size = size // 2 if kind == "halve" else size
            received.append(pltpu.VMEM((size, rows, c1), BF16))
        return sums + received + [pltpu.SemaphoreType.DMA((len(stages),))] * 2

    vmem = pl.BlockSpec(memory_space=pltpu.VMEM)
    second_out, out1, out2 = pl.pallas_call(
        functools.partial(kernel, plans, spaces, groups),
        out_shape=(
            jax.ShapeDtypeStruct((q * r, c1), BF16),
            jax.ShapeDtypeStruct((27, GROUP, c0), F32),
            jax.ShapeDtypeStruct((27 * GROUP, c1), F32),
        ),
        in_specs=[vmem] * 4,
        out_specs=(vmem,) * 3,
        scratch_shapes=[
            pltpu.VMEM((height // 2, 2, width // 2, 2 * c0), BF16),
            pltpu.VMEM((height // 2, width // 2, c1), BF16),
            pltpu.VMEM((height // 2, width // 2, c1), BF16),
            pltpu.VMEM((3, height // 4, 2, width // 2, c1), F32),
            pltpu.VMEM((q, r, c1), BF16),
            pltpu.VMEM((q, r, c1), BF16),
            pltpu.VMEM((2, height // 4, 2, width // 2, c1), F32),
            pltpu.VMEM((rows1, c1), F32),
            pltpu.VMEM((rows2, c1), F32),
            pltpu.SemaphoreType.DMA((3,)),
            pltpu.SemaphoreType.DMA((3,)),
            *[each for plan in plans for each in buffers(*plan[:2])],
        ],
        compiler_params=pltpu.CompilerParams(
            collective_id=0, has_side_effects=True, vmem_limit_bytes=50 * 1024 * 1024
        ),
    )(vol, w1, w2, up)

    own = c1 // spaces
    start = (lax.axis_index("space") % (GROUP // own)) * own if own < GROUP else 0
    units2 = out2.reshape(27, GROUP, c1)
    if own < GROUP:
        units2 = lax.dynamic_slice_in_dim(units2, start, own, 1)
        out1 = lax.dynamic_slice_in_dim(out1, start, own, 1)
    second_grad = units2.reshape(3, 3, 3, own, c1)
    first_grad = jnp.transpose(out1.reshape(3, 3, 3, own, c0), (0, 1, 2, 4, 3))
    return second_out.reshape(1, 1, q, r, c1), first_grad, second_grad


def solution(mesh):
    placed = (P("dp", "space", None, None), P(), P(), P("dp", "space", None, None, None))
    body = functools.partial(local, spaces=mesh.shape["space"], samples=mesh.shape["dp"])
    return jax.shard_map(
        body,
        mesh=mesh,
        in_specs=placed,
        out_specs=(
            P("dp", "space", None, None, None),
            P(None, None, None, None, "space"),
            P(None, None, None, "space", None),
        ),
        check_vma=False,
    )
```
